1024 devices in a mesh: rep: 4 (over y_hi), ctx: 32 (over z, y_lo), head: 8 (over x, core).
Axes of the slice: x: 4, y: 8 (y_hi: 4, y_lo: 2; y = y_hi * 2 + y_lo), z: 16, core: 2. Of those that a mesh axis runs over, the one named last changes fastest.
Arguments:
- queries: bfloat16 [98304, 8, 512], P(('rep', 'ctx', 'head')), parts along dimension 0, may hold values from -48 to 48
- keyvals: bfloat16 [98304, 8, 256], P(('rep', 'ctx', 'head')), parts along dimension 0, may hold values from -24 to 24
- doc_lengths: int32 [128], P('rep'), parts along dimension 0, may hold values from 1 to 1536, 24576 in all
Outputs:
- attended: bfloat16 [98304, 8, 512], P(('rep', 'ctx', 'head')), parts along dimension 0
The draws below stay inside these ranges and needn't reach their ends.
There are 4 independent parts, one for each index of `rep`. The reference program is written for one: setup_inputs(seed, part) draws one part's arguments, and reference() takes and returns one part's arrays. A program takes and returns all parts, laid end to end along the dimension named above; each array names one. Nothing has to cross between parts.
Inputs may be any that keep to these rules, and one draw needn't show every extreme that they name: `doc_lengths`: the documents fill the sequence in order and their lengths sum to 24576; one of them is exactly 1536 tokens long.
All inputs are finite; a program needn't handle non-finite values.
Results may differ from the reference program's by a relative error of at most 0.0037.
Values may be sent and summed in bfloat16 or wider, within the bound.
A program may use at most 32 MiB of HBM per device.

```python
import math
import jax
import jax.numpy as jnp
import numpy as np
from jax import lax

KV_HEADS = 8
GROUP = 4
HEAD_DIM = 128
STRETCH = 768
NDOCS = 32
WINDOW = 2
SEQ = 24576
MOST = 1536


def base_fields(key):
    inner = jax.random.fold_in(key, 31)
    key_draw, value_draw = jax.random.split(inner)
    shape = (SEQ, KV_HEADS, HEAD_DIM)
    key_field = jax.random.truncated_normal(key_draw, -6.0, 6.0, shape, jnp.float32)
    value_field = 4.0 * jax.random.truncated_normal(value_draw, -6.0, 6.0, shape, jnp.float32)
    return (key_field, value_field)


def draw_keyvals(key, part):
    key_field, value_field = base_fields(key)
    return jnp.concatenate([key_field, value_field], axis=-1).astype(jnp.bfloat16)


def draw_queries(key, part):
    query_key = jax.random.fold_in(key, 53)
    shape = (SEQ, KV_HEADS, GROUP, HEAD_DIM)
    query_field = jax.random.truncated_normal(query_key, -6.0, 6.0, shape, jnp.float32)
    return query_field.reshape(SEQ, KV_HEADS, GROUP * HEAD_DIM).astype(jnp.bfloat16)


def profile(count, total, bound, slope):
    portions = [(1 << 20) // math.isqrt(standing ** slope) + 1 for standing in range(2, count + 1)]
    surplus, given = total - bound - (count - 1), [1] * (count - 1)
    while surplus > 0:
        free = [i for i in range(count - 1) if given[i] < bound]
        mass, left = sum([portions[i] for i in free]), surplus
        for i in free:
            extra = min(bound - given[i], max(1, left * portions[i] // mass), surplus)
            given[i] = given[i] + extra
            surplus = surplus - extra
    return np.array([bound] + given)


def ragged_sizes(rng, amount, total, reach, skew):
    if amount == 2:
        one = jax.random.randint(rng, (), max(1, total - reach), min(reach, total - 1) + 1)
        return jnp.stack([one, total - one])
    tallies = jnp.asarray(profile(amount, total, reach, skew), jnp.int32)
    twos = (amount - 1) // 2
    source_of, sink = tallies[1:1 + 2 * twos:2], tallies[2:2 + 2 * twos:2]
    room = jnp.minimum(source_of - 1, reach - sink)
    passed = jax.random.randint(jax.random.fold_in(rng, 1), (twos,), 0, 1 << 20) % (room + 1)
    tallies = tallies.at[1:1 + 2 * twos:2].set(source_of - passed).at[2:2 + 2 * twos:2].set(sink + passed)
    return tallies[jax.random.permutation(jax.random.fold_in(rng, 2), amount)]


def setup_inputs(seed: int = 0, part: int = 0) -> dict:
    arg_keys = jax.random.split(jax.random.key(seed), 4)
    own_keys = jax.random.split(jax.random.fold_in(arg_keys[3], part), 4)
    queries = draw_queries(jax.random.fold_in(jax.random.fold_in(arg_keys[3], part), 71), part)
    keyvals = draw_keyvals(jax.random.fold_in(jax.random.fold_in(arg_keys[3], part), 71), part)
    doc_lengths = ragged_sizes(own_keys[2], NDOCS, SEQ, MOST, 2).astype(jnp.int32)
    return {"queries": queries, "keyvals": keyvals, "doc_lengths": doc_lengths}


def doc_numbers(positions, doc_ends):
    return jnp.sum((doc_ends[None, :] <= positions[:, None]).astype(jnp.int32), axis=1).astype(jnp.int32)


def reference(queries, keyvals, doc_lengths):
    seq_len = queries.shape[0]
    groups = queries.shape[1]
    pad_rows = WINDOW * STRETCH
    doc_ends = jnp.cumsum(doc_lengths).astype(jnp.int32)
    positions = jnp.arange(seq_len).astype(jnp.int32)
    doc_ids = doc_numbers(positions, doc_ends)
    padded_kv = jnp.concatenate([jnp.zeros((pad_rows, groups, 2 * HEAD_DIM), keyvals.dtype), keyvals], axis=0)
    padded_pos = jnp.concatenate([jnp.arange(pad_rows).astype(jnp.int32) - pad_rows, positions])
    padded_doc = jnp.concatenate([jnp.full((pad_rows,), -1, jnp.int32), doc_ids])
    score_scale = HEAD_DIM ** -0.5

    def one_block(block_index):
        start = (block_index * STRETCH).astype(jnp.int32)
        query_rows = lax.dynamic_slice_in_dim(queries, start, STRETCH, 0).astype(jnp.float32)
        query_rows = query_rows.reshape(STRETCH, groups, GROUP, HEAD_DIM)
        kv_block = lax.dynamic_slice_in_dim(padded_kv, start, pad_rows + STRETCH, 0).astype(jnp.float32)
        key_rows = kv_block[:, :, :HEAD_DIM]
        value_rows = kv_block[:, :, HEAD_DIM:]
        query_pos = lax.dynamic_slice_in_dim(positions, start, STRETCH, 0)
        query_doc = lax.dynamic_slice_in_dim(doc_ids, start, STRETCH, 0)
        key_pos = lax.dynamic_slice_in_dim(padded_pos, start, pad_rows + STRETCH, 0)
        key_doc = lax.dynamic_slice_in_dim(padded_doc, start, pad_rows + STRETCH, 0)
        allowed = (key_doc[None, :] == query_doc[:, None]) & (key_pos[None, :] <= query_pos[:, None])
        scores = jnp.einsum("qgjd,kgd->gjqk", query_rows, key_rows) * score_scale
        scores = jnp.where(allowed[None, None], scores, -1e30)
        row_max = jnp.max(scores, axis=-1, keepdims=True)
        exp_scores = jnp.where(allowed[None, None], jnp.exp(scores - row_max), 0.0)
        row_total = jnp.sum(exp_scores, axis=-1, keepdims=True)
        weights = lax.optimization_barrier(exp_scores.astype(jnp.bfloat16)).astype(jnp.float32)
        mixed_rows = jnp.einsum("gjqk,kgd->gjqd", weights, value_rows) / row_total
        mixed_rows = jnp.transpose(mixed_rows, (2, 0, 1, 3)).reshape(STRETCH, groups, GROUP * HEAD_DIM)
        return mixed_rows.astype(jnp.bfloat16)

    blocks = lax.map(one_block, jnp.arange(seq_len // STRETCH).astype(jnp.int32))
    return blocks.reshape(seq_len, groups, GROUP * HEAD_DIM)
```

```python
import functools

import jax
import jax.numpy as jnp
from jax import lax
from jax.experimental import pallas as pl
from jax.experimental.pallas import tpu as pltpu
from jax.sharding import PartitionSpec as P

GROUP = 4
HEAD_DIM = 128
REACH = 2
TILE = 128
MASKED = -1e30
LOG2E = 1.4426950408889634
MESH = pl.DeviceIdType.MESH


def spread(step):
    return 4 + (1 - 2 * (step % 2)) * ((step + 1) // 2)


def attention_kernel(
    heads, ctxs, lengths, q_in, kv_in, out, window, q_rows, first_key, scores, mixed,
    kv_send, kv_recv, q_send, q_recv, z_send, z_recv, y_send, y_recv, o_send, o_recv, own_sem,
):
    rows = q_in.shape[1]
    block = heads * rows
    me = lax.axis_index("head")
    ctx = lax.axis_index("ctx")
    odd = ctx % 2
    far = (ctx + 2) % ctxs
    back = (ctx + ctxs - 2) % ctxs
    beside = ctx + 1 - 2 * odd
    span = REACH * block + rows
    tiles = pl.cdiv(span, TILE)
    pad = tiles * TILE - span

    def key_rows(which, piece):
        return window.at[pl.ds(pl.multiple_of(pad + which * block + piece * rows, 32), rows), :]

    def query_rows(piece):
        return q_rows.at[pl.ds(pl.multiple_of(piece * rows, 32), rows), :]

    def kv_copy(dest, source):
        return pltpu.make_async_remote_copy(
            src_ref=kv_in.at[dest], dst_ref=key_rows(REACH, source),
            send_sem=kv_send.at[dest], recv_sem=kv_recv.at[source],
            device_id={"head": dest}, device_id_type=MESH,
        )

    def q_copy(dest, source):
        return pltpu.make_async_remote_copy(
            src_ref=q_in.at[dest], dst_ref=query_rows(source),
            send_sem=q_send.at[dest], recv_sem=q_recv.at[source],
            device_id={"head": dest}, device_id_type=MESH,
        )

    def z_copy(piece):
        return pltpu.make_async_remote_copy(
            src_ref=key_rows(REACH, piece), dst_ref=key_rows(0, piece),
            send_sem=z_send.at[piece], recv_sem=z_recv.at[piece],
            device_id={"ctx": far}, device_id_type=MESH,
        )

    def y_copy(piece):
        return pltpu.make_async_remote_copy(
            src_ref=key_rows(REACH * (1 - odd), piece), dst_ref=key_rows(1, piece),
            send_sem=y_send.at[piece], recv_sem=y_recv.at[piece],
            device_id={"ctx": beside}, device_id_type=MESH,
        )

    def o_copy(dest, source):
        return pltpu.make_async_remote_copy(
            src_ref=mixed.at[dest], dst_ref=out.at[source],
            send_sem=o_send.at[dest], recv_sem=o_recv.at[source],
            device_id={"head": dest}, device_id_type=MESH,
        )

    own_kv = pltpu.make_async_copy(kv_in.at[me], key_rows(REACH, me), own_sem.at[0])
    own_q = pltpu.make_async_copy(q_in.at[me], query_rows(me), own_sem.at[1])
    own_kv.start()
    own_q.start()

    barrier = pltpu.get_barrier_semaphore()
    for step in range(1, heads):
        peer = (me + step) % heads
        pl.semaphore_signal(barrier, inc=1, device_id={"head": peer}, device_id_type=MESH)
    for peer in (far, back, beside):
        pl.semaphore_signal(barrier, inc=1, device_id={"ctx": peer}, device_id_type=MESH)
    pl.semaphore_wait(barrier, heads + 2)

    @pl.loop(0, heads - 1)
    def _(step):
        kv_copy((me + spread(step)) % heads, me).start()

    @pl.loop(0, heads - 1)
    def _(step):
        q_copy((me + spread(step)) % heads, me).start()

    window[:pad, :] = jnp.zeros((pad, window.shape[1]), window.dtype)

    @pl.loop(0, heads)
    def _(chunk):
        place = lax.broadcasted_iota(jnp.int32, (rows, TILE), 0) + (ctx * block + chunk * rows)
        start = jnp.zeros((rows, TILE), jnp.int32)
        end = jnp.int32(0)
        for doc in range(lengths.shape[0]):
            end = end + lengths[doc]
            start = jnp.where(place >= end, end, start)
        first_key[chunk] = start - ((ctx - REACH) * block + chunk * rows - pad)

    own_kv.wait()

    def pass_on(piece):
        z_copy(piece).start()

        @pl.when(odd == 0)
        def _():
            y_copy(piece).start()

    pass_on(me)

    @pl.loop(0, heads - 1)
    def _(step):
        piece = (me + heads - spread(step)) % heads
        kv_copy(piece, piece).wait_recv()
        pass_on(piece)

    @pl.loop(0, heads)
    def _(step):
        piece = (me + heads - spread(heads - 1 - step)) % heads
        z_copy(piece).wait_recv()

        @pl.when(odd == 1)
        def _():
            y_copy(piece).start()

    @pl.loop(0, heads)
    def _(step):
        piece = (me + heads - spread(heads - 1 - step)) % heads
        y_copy(piece).wait_recv()

    own_q.wait()
    sharpness = HEAD_DIM ** -0.5 * LOG2E

    @pl.loop(0, heads)
    def _(step):
        chunk = (me + spread(step)) % heads

        @pl.when(step < heads - 1)
        def _():
            q_copy(chunk, chunk).wait_recv()

        packed = query_rows(chunk)[...]
        stacked = jnp.concatenate(
            [packed[:, j * HEAD_DIM:(j + 1) * HEAD_DIM] for j in range(GROUP)], axis=0
        )
        base = chunk * rows
        lowest = first_key[chunk]
        lane = lax.broadcasted_iota(jnp.int32, (rows, TILE), 1)
        row = lax.broadcasted_iota(jnp.int32, (rows, TILE), 0)
        top = None
        for tile in range(tiles):
            keys = window[pl.ds(pl.multiple_of(base + tile * TILE, 32), TILE), :HEAD_DIM]
            part = lax.dot_general(
                stacked, keys, (((1,), (1,)), ((), ())), preferred_element_type=jnp.float32
            )
            here = lane + tile * TILE
            kept = here >= lowest
            if (tile + 1) * TILE > pad + REACH * block:
                kept = kept & (here <= row + (pad + REACH * block))
            part = jnp.where(kept[None], part.reshape(GROUP, rows, TILE), MASKED)
            part = part.reshape(GROUP * rows, TILE)
            scores[tile] = part
            top = part if top is None else jnp.maximum(top, part)
        top = jnp.max(top, axis=1, keepdims=True)
        total = None
        result = None
        for tile in range(0, tiles, 2):
            weights = []
            for half in range(tile, min(tile + 2, tiles)):
                part = jnp.exp2((scores[half] - top) * sharpness)
                total = part if total is None else total + part
                weights.append(part.astype(jnp.bfloat16))
            weights = jnp.concatenate(weights, axis=1)
            width = weights.shape[1]
            values = window[pl.ds(pl.multiple_of(base + tile * TILE, 32), width), HEAD_DIM:]
            part = jnp.dot(weights, values, preferred_element_type=jnp.float32)
            result = part if result is None else result + part
        total = jnp.sum(total, axis=1, keepdims=True)
        result = (result / total).astype(jnp.bfloat16)
        for j in range(GROUP):
            mixed[chunk, :, j * HEAD_DIM:(j + 1) * HEAD_DIM] = result[j * rows:(j + 1) * rows]

        @pl.when(step < heads - 1)
        def _():
            o_copy(chunk, me).start()

    own_out = pltpu.make_async_copy(mixed.at[me], out.at[me], own_sem.at[2])
    own_out.start()

    @pl.loop(0, heads - 1)
    def _(step):
        dest = (me + spread(step)) % heads
        kv_copy(dest, me).wait_send()
        q_copy(dest, me).wait_send()
        o_copy(dest, me).wait_send()
        o_copy(dest, dest).wait_recv()

    @pl.loop(0, heads)
    def _(piece):
        z_copy(piece).wait_send()
        y_copy(piece).wait_send()

    own_out.wait()


def local(heads, ctxs, queries, keyvals, doc_lengths):
    q_in = jnp.transpose(queries, (1, 0, 2))
    kv_in = jnp.transpose(keyvals, (1, 0, 2))
    rows = queries.shape[0]
    block = heads * rows
    span = REACH * block + rows
    tiles = pl.cdiv(span, TILE)
    pad = tiles * TILE - span
    dma = pltpu.SemaphoreType.DMA((heads,))
    gathered = pl.pallas_call(
        functools.partial(attention_kernel, heads, ctxs),
        out_shape=jax.ShapeDtypeStruct(q_in.shape, jnp.bfloat16),
        in_specs=[
            pl.BlockSpec(memory_space=pltpu.SMEM),
            pl.BlockSpec(memory_space=pl.ANY),
            pl.BlockSpec(memory_space=pl.ANY),
        ],
        out_specs=pl.BlockSpec(memory_space=pl.ANY),
        scratch_shapes=[
            pltpu.VMEM((pad + (REACH + 1) * block, keyvals.shape[2]), jnp.bfloat16),
            pltpu.VMEM((block, queries.shape[2]), jnp.bfloat16),
            pltpu.VMEM((heads, rows, TILE), jnp.int32),
            pltpu.VMEM((tiles, GROUP * rows, TILE), jnp.float32),
            pltpu.VMEM((heads, rows, queries.shape[2]), jnp.bfloat16),
            dma, dma, dma, dma, dma, dma, dma, dma, dma, dma,
            pltpu.SemaphoreType.DMA((3,)),
        ],
        compiler_params=pltpu.CompilerParams(collective_id=0, has_side_effects=True),
    )(doc_lengths, q_in, kv_in)
    return jnp.transpose(gathered, (1, 0, 2))


def solution(mesh):
    spec = P(("rep", "ctx", "head"), None, None)
    return jax.shard_map(
        functools.partial(local, mesh.shape["head"], mesh.shape["ctx"]),
        mesh=mesh,
        in_specs=(spec, spec, P("rep")),
        out_specs=spec,
        check_vma=False,
    )
```

```python
import functools

import jax
import jax.numpy as jnp
from jax import lax
from jax.experimental import pallas as pl
from jax.experimental.pallas import tpu as pltpu
from jax.sharding import PartitionSpec as P

GROUP = 4
HEAD_DIM = 128
REACH = 2
TILE = 128
MASKED = -1e30
LOG2E = 1.4426950408889634
MESH = pl.DeviceIdType.MESH


NEAR_FIRST = (6, 3, 5, 2, 4, 1, 0)


def peer_at(me, step, heads, way):
    pair = step // 2
    chips = heads // 2
    distance = chips // 2 + (1 - 2 * (pair % 2)) * ((pair + 1) // 2)
    flip = (step + pair // 3) % 2
    return 2 * ((me // 2 + chips + way * distance) % chips) + (me + flip) % 2


def attention_kernel(
    heads, ctxs, doc_lengths, q_in, kv_in, out, window, q_rows, lengths, first_key, scores_a, scores_b, tops, mixed,
    kv_send, kv_recv, q_send, q_recv, z_send, z_recv, y_send, y_recv, o_send, o_recv, own_sem,
):
    rows = q_in.shape[1]
    block = heads * rows
    me = lax.axis_index("head")
    ctx = lax.axis_index("ctx")
    odd = ctx % 2
    far = (ctx + 2) % ctxs
    back = (ctx + ctxs - 2) % ctxs
    beside = ctx + 1 - 2 * odd
    span = REACH * block + rows
    tiles = pl.cdiv(span, TILE)
    pad = tiles * TILE - span

    def key_rows(which, piece):
        return window.at[pl.ds(pl.multiple_of(pad + which * block + piece * rows, 32), rows), :]

    def query_rows(piece):
        return q_rows.at[pl.ds(pl.multiple_of(piece * rows, 32), rows), :]

    def kv_copy(dest, source):
        return pltpu.make_async_remote_copy(
            src_ref=kv_in.at[dest], dst_ref=key_rows(REACH, source),
            send_sem=kv_send.at[dest], recv_sem=kv_recv.at[source],
            device_id={"head": dest}, device_id_type=MESH,
        )

    def q_copy(dest, source):
        return pltpu.make_async_remote_copy(
            src_ref=q_in.at[dest], dst_ref=query_rows(source),
            send_sem=q_send.at[dest], recv_sem=q_recv.at[source],
            device_id={"head": dest}, device_id_type=MESH,
        )

    def z_copy(piece):
        return pltpu.make_async_remote_copy(
            src_ref=key_rows(REACH, piece), dst_ref=key_rows(0, piece),
            send_sem=z_send.at[piece], recv_sem=z_recv.at[piece],
            device_id={"ctx": far}, device_id_type=MESH,
        )

    def y_copy(piece):
        return pltpu.make_async_remote_copy(
            src_ref=key_rows(REACH * (1 - odd), piece), dst_ref=key_rows(1, piece),
            send_sem=y_send.at[piece], recv_sem=y_recv.at[piece],
            device_id={"ctx": beside}, device_id_type=MESH,
        )

    def o_copy(dest, source):
        return pltpu.make_async_remote_copy(
            src_ref=mixed.at[dest], dst_ref=out.at[source],
            send_sem=o_send.at[dest], recv_sem=o_recv.at[source],
            device_id={"head": dest}, device_id_type=MESH,
        )

    own_kv = pltpu.make_async_copy(kv_in.at[me], key_rows(REACH, me), own_sem.at[0])
    own_q = pltpu.make_async_copy(q_in.at[me], query_rows(me), own_sem.at[1])
    lengths_in = pltpu.make_async_copy(doc_lengths, lengths, own_sem.at[3])
    lengths_in.start()
    own_kv.start()
    own_q.start()

    barrier = pltpu.get_barrier_semaphore()
    for step in range(1, heads):
        peer = (me + step) % heads
        pl.semaphore_signal(barrier, inc=1, device_id={"head": peer}, device_id_type=MESH)
    for peer in (back, beside):
        pl.semaphore_signal(barrier, inc=1, device_id={"ctx": peer}, device_id_type=MESH)
    pl.semaphore_wait(barrier, heads + 1)

    for step in NEAR_FIRST:
        kv_copy(peer_at(me, step, heads, 1), me).start()

    @pl.loop(0, heads - 1)
    def _(step):
        q_copy(peer_at(me, step, heads, 1), me).start()

    window[:pad, :] = jnp.zeros((pad, window.shape[1]), window.dtype)

    lengths_in.wait()

    @pl.loop(0, heads)
    def _(chunk):
        place = lax.broadcasted_iota(jnp.int32, (rows, TILE), 0) + (ctx * block + chunk * rows)
        start = jnp.zeros((rows, TILE), jnp.int32)
        end = jnp.int32(0)
        for doc in range(lengths.shape[0]):
            end = end + lengths[doc]
            start = jnp.where(place >= end, end, start)
        first_key[chunk] = start - ((ctx - REACH) * block + chunk * rows - pad)

    own_kv.wait()

    def pass_on(piece):
        z_copy(piece).start()

        @pl.when(odd == 0)
        def _():
            y_copy(piece).start()

    pass_on(me)
    for step in NEAR_FIRST:
        piece = peer_at(me, step, heads, -1)
        kv_copy(piece, piece).wait_recv()
        pass_on(piece)

    for step in (heads - 1, *NEAR_FIRST):
        piece = peer_at(me, step, heads, -1)
        z_copy(piece).wait_recv()

        @pl.when(odd == 1)
        def _():
            y_copy(piece).start()

    @pl.loop(0, heads)
    def _(piece):
        y_copy(piece).wait_recv()

    own_q.wait()
    sharpness = HEAD_DIM ** -0.5 * LOG2E

    def chunk_of(step):
        return peer_at(me, step, heads, 1)

    def score(chunk, scores):
        packed = query_rows(chunk)[...]
        stacked = jnp.concatenate(
            [packed[:, j * HEAD_DIM:(j + 1) * HEAD_DIM] for j in range(GROUP)], axis=0
        )
        base = chunk * rows
        lowest = first_key[chunk]
        lane = lax.broadcasted_iota(jnp.int32, (rows, TILE), 1)
        row = lax.broadcasted_iota(jnp.int32, (rows, TILE), 0)
        top = None
        for tile in range(0, tiles, 2):
            width = min(2, tiles - tile) * TILE
            keys = window[pl.ds(pl.multiple_of(base + tile * TILE, 32), width), :HEAD_DIM]
            both = lax.dot_general(
                stacked, keys, (((1,), (1,)), ((), ())), preferred_element_type=jnp.float32
            )
            for half in range(width // TILE):
                part = both[:, half * TILE:(half + 1) * TILE]
                here = lane + (tile + half) * TILE
                kept = here >= lowest
                if (tile + half + 1) * TILE > pad + REACH * block:
                    kept = kept & (here <= row + (pad + REACH * block))
                part = jnp.where(kept[None], part.reshape(GROUP, rows, TILE), MASKED)
                part = part.reshape(GROUP * rows, TILE)
                scores[tile + half] = part
                top = part if top is None else jnp.maximum(top, part)
        return jnp.max(top, axis=1, keepdims=True)

    def mix(chunk, scores, top):
        base = chunk * rows
        total = None
        weights = []
        for tile in range(tiles):
            part = jnp.exp2((scores[tile] - top) * sharpness)
            total = part if total is None else total + part
            weights.append(part.astype(jnp.bfloat16))
        values = window[pl.ds(pl.multiple_of(base, 32), tiles * TILE), HEAD_DIM:]
        result = jnp.dot(
            jnp.concatenate(weights, axis=1), values, preferred_element_type=jnp.float32
        )
        total = jnp.sum(total, axis=1, keepdims=True)
        result = (result / total).astype(jnp.bfloat16)
        for j in range(GROUP):
            mixed[chunk, :, j * HEAD_DIM:(j + 1) * HEAD_DIM] = result[j * rows:(j + 1) * rows]

    def await_queries(step):
        @pl.when(step < heads - 1)
        def _():
            source = chunk_of(step)
            q_copy(source, source).wait_recv()

    def send_mixed(step):
        @pl.when(step < heads - 1)
        def _():
            o_copy(chunk_of(step), me).start()

    await_queries(0)
    tops[0] = score(chunk_of(0), scores_a)

    @pl.loop(0, heads, step=2)
    def _(step):
        await_queries(step + 1)
        tops[1] = score(chunk_of(step + 1), scores_b)
        mix(chunk_of(step), scores_a, tops[0])
        send_mixed(step)
        after = jnp.minimum(step + 2, heads - 1)
        await_queries(step + 2)
        tops[0] = score(chunk_of(after), scores_a)
        mix(chunk_of(step + 1), scores_b, tops[1])
        send_mixed(step + 1)

    own_out = pltpu.make_async_copy(mixed.at[me], out.at[me], own_sem.at[2])
    own_out.start()

    @pl.loop(0, heads - 1)
    def _(step):
        dest = (me + 1 + step) % heads
        kv_copy(dest, me).wait_send()
        q_copy(dest, me).wait_send()
        o_copy(dest, me).wait_send()
        o_copy(dest, dest).wait_recv()

    @pl.loop(0, heads)
    def _(piece):
        z_copy(piece).wait_send()
        y_copy(piece).wait_send()

    own_out.wait()


def local(heads, ctxs, queries, keyvals, doc_lengths):
    q_in = jnp.transpose(queries, (1, 0, 2))
    kv_in = jnp.transpose(keyvals, (1, 0, 2))
    rows = queries.shape[0]
    block = heads * rows
    span = REACH * block + rows
    tiles = pl.cdiv(span, TILE)
    pad = tiles * TILE - span
    dma = pltpu.SemaphoreType.DMA((heads,))
    gathered = pl.pallas_call(
        functools.partial(attention_kernel, heads, ctxs),
        out_shape=jax.ShapeDtypeStruct(q_in.shape, jnp.bfloat16),
        in_specs=[
            pl.BlockSpec(memory_space=pltpu.HBM),
            pl.BlockSpec(memory_space=pl.ANY),
            pl.BlockSpec(memory_space=pl.ANY),
        ],
        out_specs=pl.BlockSpec(memory_space=pl.ANY),
        scratch_shapes=[
            pltpu.VMEM((pad + (REACH + 1) * block, keyvals.shape[2]), jnp.bfloat16),
            pltpu.VMEM((block, queries.shape[2]), jnp.bfloat16),
            pltpu.SMEM(doc_lengths.shape, jnp.int32),
            pltpu.VMEM((heads, rows, TILE), jnp.int32),
            pltpu.VMEM((tiles, GROUP * rows, TILE), jnp.float32),
            pltpu.VMEM((tiles, GROUP * rows, TILE), jnp.float32),
            pltpu.VMEM((2, GROUP * rows, 1), jnp.float32),
            pltpu.VMEM((heads, rows, queries.shape[2]), jnp.bfloat16),
            dma, dma, dma, dma, dma, dma, dma, dma, dma, dma,
            pltpu.SemaphoreType.DMA((4,)),
        ],
        compiler_params=pltpu.CompilerParams(collective_id=0, has_side_effects=True, vmem_limit_bytes=20 << 20),
    )(pltpu.with_memory_space_constraint(doc_lengths, pltpu.HBM), q_in, kv_in)
    return jnp.transpose(gathered, (1, 0, 2))


def solution(mesh):
    spec = P(("rep", "ctx", "head"), None, None)
    return jax.shard_map(
        functools.partial(local, mesh.shape["head"], mesh.shape["ctx"]),
        mesh=mesh,
        in_specs=(spec, spec, P("rep")),
        out_specs=spec,
        check_vma=False,
    )
```

```python
import functools

import jax
import jax.numpy as jnp
from jax import lax
from jax.experimental import pallas as pl
from jax.experimental.pallas import tpu as pltpu
from jax.sharding import PartitionSpec as P

GROUP = 4
HEAD_DIM = 128
REACH = 2
TILE = 128
MASKED = -1e30
LOG2E = 1.4426950408889634
MESH = pl.DeviceIdType.MESH


NEAR_FIRST = (6, 3, 5, 2, 4, 1, 0)


def peer_at(me, step, heads, way):
    pair = step // 2
    chips = heads // 2
    distance = chips // 2 + (1 - 2 * (pair % 2)) * ((pair + 1) // 2)
    flip = (step + pair // 3) % 2
    return 2 * ((me // 2 + chips + way * distance) % chips) + (me + flip) % 2


def attention_kernel(
    heads, ctxs, doc_lengths, q_in, kv_in, out, window, q_rows, lengths, first_key, scores_a, scores_b, tops, mixed,
    kv_send, kv_recv, q_send, q_recv, z_send, z_recv, y_send, y_recv, o_send, o_recv, own_sem,
):
    rows = q_in.shape[1]
    block = heads * rows
    me = lax.axis_index("head")
    ctx = lax.axis_index("ctx")
    odd = ctx % 2
    first = ctx < REACH
    last = ctx >= ctxs - REACH
    far = (ctx + REACH) % ctxs
    back = (ctx + ctxs - REACH) % ctxs
    beside = ctx + 1 - 2 * odd
    span = REACH * block + rows
    tiles = pl.cdiv(span, TILE)
    pad = tiles * TILE - span

    def key_rows(which, piece):
        return window.at[pl.ds(pl.multiple_of(pad + which * block + piece * rows, 32), rows), :]

    def query_rows(piece):
        return q_rows.at[pl.ds(pl.multiple_of(piece * rows, 32), rows), :]

    def kv_copy(dest, source):
        return pltpu.make_async_remote_copy(
            src_ref=kv_in.at[dest], dst_ref=key_rows(REACH, source),
            send_sem=kv_send.at[dest], recv_sem=kv_recv.at[source],
            device_id={"head": dest}, device_id_type=MESH,
        )

    def q_copy(dest, source):
        return pltpu.make_async_remote_copy(
            src_ref=q_in.at[dest], dst_ref=query_rows(source),
            send_sem=q_send.at[dest], recv_sem=q_recv.at[source],
            device_id={"head": dest}, device_id_type=MESH,
        )

    def z_copy(piece):
        return pltpu.make_async_remote_copy(
            src_ref=key_rows(REACH, piece), dst_ref=key_rows(0, piece),
            send_sem=z_send.at[piece], recv_sem=z_recv.at[piece],
            device_id={"ctx": far}, device_id_type=MESH,
        )

    def y_copy(piece):
        return pltpu.make_async_remote_copy(
            src_ref=key_rows(REACH * (1 - odd), piece), dst_ref=key_rows(1, piece),
            send_sem=y_send.at[piece], recv_sem=y_recv.at[piece],
            device_id={"ctx": beside}, device_id_type=MESH,
        )

    def o_copy(dest, source):
        return pltpu.make_async_remote_copy(
            src_ref=mixed.at[dest], dst_ref=out.at[source],
            send_sem=o_send.at[dest], recv_sem=o_recv.at[source],
            device_id={"head": dest}, device_id_type=MESH,
        )

    own_kv = pltpu.make_async_copy(kv_in.at[me], key_rows(REACH, me), own_sem.at[0])
    own_q = pltpu.make_async_copy(q_in.at[me], query_rows(me), own_sem.at[1])
    lengths_in = pltpu.make_async_copy(doc_lengths, lengths, own_sem.at[3])
    lengths_in.start()
    own_kv.start()
    own_q.start()

    barrier = pltpu.get_barrier_semaphore()
    for step in range(1, heads):
        peer = (me + step) % heads
        pl.semaphore_signal(barrier, inc=1, device_id={"head": peer}, device_id_type=MESH)
    pl.semaphore_signal(barrier, inc=1, device_id={"ctx": beside}, device_id_type=MESH)

    @pl.when(jnp.logical_not(first))
    def _():
        pl.semaphore_signal(barrier, inc=1, device_id={"ctx": back}, device_id_type=MESH)

    window[:pad, :] = jnp.zeros((pad, window.shape[1]), window.dtype)

    @pl.when(first)
    def _():
        window[pad:pad + block, :] = jnp.zeros((block, window.shape[1]), window.dtype)

    @pl.when(ctx == 0)
    def _():
        window[pad + block:pad + REACH * block, :] = jnp.zeros(
            (block, window.shape[1]), window.dtype
        )

    pl.semaphore_wait(barrier, heads + 1 - (ctx + REACH) // ctxs)

    for step in NEAR_FIRST:
        kv_copy(peer_at(me, step, heads, 1), me).start()

    @pl.loop(0, heads - 1)
    def _(step):
        q_copy(peer_at(me, step, heads, 1), me).start()

    lengths_in.wait()

    @pl.loop(0, heads)
    def _(chunk):
        place = lax.broadcasted_iota(jnp.int32, (rows, TILE), 0) + (ctx * block + chunk * rows)
        start = jnp.zeros((rows, TILE), jnp.int32)
        end = jnp.int32(0)
        for doc in range(lengths.shape[0]):
            end = end + lengths[doc]
            start = jnp.where(place >= end, end, start)
        first_key[chunk] = start - ((ctx - REACH) * block + chunk * rows - pad)

    own_kv.wait()

    def pass_on(piece):
        @pl.when(jnp.logical_not(last))
        def _():
            z_copy(piece).start()

        @pl.when(odd == 0)
        def _():
            y_copy(piece).start()

    pass_on(me)
    for step in NEAR_FIRST:
        piece = peer_at(me, step, heads, -1)
        kv_copy(piece, piece).wait_recv()
        pass_on(piece)

    @pl.when(jnp.logical_not(first))
    def _():
        for step in (heads - 1, *NEAR_FIRST):
            piece = peer_at(me, step, heads, -1)
            z_copy(piece).wait_recv()

            @pl.when(odd == 1)
            def _():
                y_copy(piece).start()

    @pl.when(ctx >= 1)
    def _():
        @pl.loop(0, heads)
        def _(piece):
            y_copy(piece).wait_recv()

    own_q.wait()
    sharpness = HEAD_DIM ** -0.5 * LOG2E

    def chunk_of(step):
        return peer_at(me, step, heads, 1)

    def score(chunk, scores):
        packed = query_rows(chunk)[...]
        stacked = jnp.concatenate(
            [packed[:, j * HEAD_DIM:(j + 1) * HEAD_DIM] for j in range(GROUP)], axis=0
        )
        base = chunk * rows
        lowest = first_key[chunk]
        lane = lax.broadcasted_iota(jnp.int32, (rows, TILE), 1)
        row = lax.broadcasted_iota(jnp.int32, (rows, TILE), 0)
        top = None
        for tile in range(0, tiles, 2):
            width = min(2, tiles - tile) * TILE
            keys = window[pl.ds(pl.multiple_of(base + tile * TILE, 32), width), :HEAD_DIM]
            both = lax.dot_general(
                stacked, keys, (((1,), (1,)), ((), ())), preferred_element_type=jnp.float32
            )
            for half in range(width // TILE):
                part = both[:, half * TILE:(half + 1) * TILE]
                here = lane + (tile + half) * TILE
                kept = here >= lowest
                if (tile + half + 1) * TILE > pad + REACH * block:
                    kept = kept & (here <= row + (pad + REACH * block))
                part = jnp.where(kept[None], part.reshape(GROUP, rows, TILE), MASKED)
                part = part.reshape(GROUP * rows, TILE)
                scores[tile + half] = part
                top = part if top is None else jnp.maximum(top, part)
        return jnp.max(top, axis=1, keepdims=True)

    def mix(chunk, scores, top):
        base = chunk * rows
        total = None
        weights = []
        for tile in range(tiles):
            part = jnp.exp2((scores[tile] - top) * sharpness)
            total = part if total is None else total + part
            weights.append(part.astype(jnp.bfloat16))
        values = window[pl.ds(pl.multiple_of(base, 32), tiles * TILE), HEAD_DIM:]
        result = jnp.dot(
            jnp.concatenate(weights, axis=1), values, preferred_element_type=jnp.float32
        )
        total = jnp.sum(total, axis=1, keepdims=True)
        result = (result / total).astype(jnp.bfloat16)
        for j in range(GROUP):
            mixed[chunk, :, j * HEAD_DIM:(j + 1) * HEAD_DIM] = result[j * rows:(j + 1) * rows]

    def await_queries(step):
        @pl.when(step < heads - 1)
        def _():
            source = chunk_of(step)
            q_copy(source, source).wait_recv()

    def send_mixed(step):
        @pl.when(step < heads - 1)
        def _():
            o_copy(chunk_of(step), me).start()

    await_queries(0)
    tops[0] = score(chunk_of(0), scores_a)

    @pl.loop(0, heads, step=2)
    def _(step):
        await_queries(step + 1)
        tops[1] = score(chunk_of(step + 1), scores_b)
        mix(chunk_of(step), scores_a, tops[0])
        send_mixed(step)
        after = jnp.minimum(step + 2, heads - 1)
        await_queries(step + 2)
        tops[0] = score(chunk_of(after), scores_a)
        mix(chunk_of(step + 1), scores_b, tops[1])
        send_mixed(step + 1)

    own_out = pltpu.make_async_copy(mixed.at[me], out.at[me], own_sem.at[2])
    own_out.start()

    @pl.loop(0, heads - 1)
    def _(step):
        dest = (me + 1 + step) % heads
        kv_copy(dest, me).wait_send()
        q_copy(dest, me).wait_send()
        o_copy(dest, me).wait_send()
        o_copy(dest, dest).wait_recv()

    @pl.when(jnp.logical_not(last))
    def _():
        @pl.loop(0, heads)
        def _(piece):
            z_copy(piece).wait_send()

    @pl.when(ctx != 1)
    def _():
        @pl.loop(0, heads)
        def _(piece):
            y_copy(piece).wait_send()

    own_out.wait()


def local(heads, ctxs, queries, keyvals, doc_lengths):
    q_in = jnp.transpose(queries, (1, 0, 2))
    kv_in = jnp.transpose(keyvals, (1, 0, 2))
    rows = queries.shape[0]
    block = heads * rows
    span = REACH * block + rows
    tiles = pl.cdiv(span, TILE)
    pad = tiles * TILE - span
    dma = pltpu.SemaphoreType.DMA((heads,))
    gathered = pl.pallas_call(
        functools.partial(attention_kernel, heads, ctxs),
        out_shape=jax.ShapeDtypeStruct(q_in.shape, jnp.bfloat16),
        in_specs=[
            pl.BlockSpec(memory_space=pltpu.HBM),
            pl.BlockSpec(memory_space=pl.ANY),
            pl.BlockSpec(memory_space=pl.ANY),
        ],
        out_specs=pl.BlockSpec(memory_space=pl.ANY),
        scratch_shapes=[
            pltpu.VMEM((pad + (REACH + 1) * block, keyvals.shape[2]), jnp.bfloat16),
            pltpu.VMEM((block, queries.shape[2]), jnp.bfloat16),
            pltpu.SMEM(doc_lengths.shape, jnp.int32),
            pltpu.VMEM((heads, rows, TILE), jnp.int32),
            pltpu.VMEM((tiles, GROUP * rows, TILE), jnp.float32),
            pltpu.VMEM((tiles, GROUP * rows, TILE), jnp.float32),
            pltpu.VMEM((2, GROUP * rows, 1), jnp.float32),
            pltpu.VMEM((heads, rows, queries.shape[2]), jnp.bfloat16),
            dma, dma, dma, dma, dma, dma, dma, dma, dma, dma,
            pltpu.SemaphoreType.DMA((4,)),
        ],
        compiler_params=pltpu.CompilerParams(collective_id=0, has_side_effects=True, vmem_limit_bytes=20 << 20),
    )(pltpu.with_memory_space_constraint(doc_lengths, pltpu.HBM), q_in, kv_in)
    return jnp.transpose(gathered, (1, 0, 2))


def solution(mesh):
    spec = P(("rep", "ctx", "head"), None, None)
    return jax.shard_map(
        functools.partial(local, mesh.shape["head"], mesh.shape["ctx"]),
        mesh=mesh,
        in_specs=(spec, spec, P("rep")),
        out_specs=spec,
        check_vma=False,
    )
```

```python
import functools

import jax
import jax.numpy as jnp
from jax import lax
from jax.experimental import pallas as pl
from jax.experimental.pallas import tpu as pltpu
from jax.sharding import PartitionSpec as P

GROUP = 4
HEAD_DIM = 128
REACH = 2
TILE = 128
MASKED = -1e30
LOG2E = 1.4426950408889634
MESH = pl.DeviceIdType.MESH


NEAR_FIRST = (6, 3, 5, 2, 4, 1, 0)


def peer_at(me, step, heads, way):
    pair = step // 2
    chips = heads // 2
    distance = chips // 2 + (1 - 2 * (pair % 2)) * ((pair + 1) // 2)
    flip = (step + pair // 3) % 2
    return 2 * ((me // 2 + chips + way * distance) % chips) + (me + flip) % 2


def attention_kernel(
    heads, ctxs, doc_lengths, q_hbm, kv_hbm, out, q_raw, kv_raw, q_in, kv_in, window, q_rows, lengths, first_key, scores_a, scores_b, tops, mixed,
    kv_send, kv_recv, q_send, q_recv, z_send, z_recv, y_send, y_recv, o_send, o_recv, own_sem,
):
    rows = q_in.shape[1]
    block = heads * rows
    me = lax.axis_index("head")
    ctx = lax.axis_index("ctx")
    odd = ctx % 2
    first = ctx < REACH
    last = ctx >= ctxs - REACH
    far = (ctx + REACH) % ctxs
    back = (ctx + ctxs - REACH) % ctxs
    beside = ctx + 1 - 2 * odd
    span = REACH * block + rows
    tiles = pl.cdiv(span, TILE)
    pad = tiles * TILE - span

    def key_rows(which, piece):
        return window.at[pl.ds(pl.multiple_of(pad + which * block + piece * rows, 32), rows), :]

    def query_rows(piece):
        return q_rows.at[pl.ds(pl.multiple_of(piece * rows, 32), rows), :]

    def kv_copy(dest, source):
        return pltpu.make_async_remote_copy(
            src_ref=kv_in.at[dest], dst_ref=key_rows(REACH, source),
            send_sem=kv_send.at[dest], recv_sem=kv_recv.at[source],
            device_id={"head": dest}, device_id_type=MESH,
        )

    def q_copy(dest, source):
        return pltpu.make_async_remote_copy(
            src_ref=q_in.at[dest], dst_ref=query_rows(source),
            send_sem=q_send.at[dest], recv_sem=q_recv.at[source],
            device_id={"head": dest}, device_id_type=MESH,
        )

    def z_copy(piece):
        return pltpu.make_async_remote_copy(
            src_ref=key_rows(REACH, piece), dst_ref=key_rows(0, piece),
            send_sem=z_send.at[piece], recv_sem=z_recv.at[piece],
            device_id={"ctx": far}, device_id_type=MESH,
        )

    def y_copy(piece):
        return pltpu.make_async_remote_copy(
            src_ref=key_rows(REACH * (1 - odd), piece), dst_ref=key_rows(1, piece),
            send_sem=y_send.at[piece], recv_sem=y_recv.at[piece],
            device_id={"ctx": beside}, device_id_type=MESH,
        )

    def o_copy(dest, source):
        return pltpu.make_async_remote_copy(
            src_ref=mixed.at[dest], dst_ref=out.at[source],
            send_sem=o_send.at[dest], recv_sem=o_recv.at[source],
            device_id={"head": dest}, device_id_type=MESH,
        )

    own_kv = pltpu.make_async_copy(kv_in.at[me], key_rows(REACH, me), own_sem.at[0])
    own_q = pltpu.make_async_copy(q_in.at[me], query_rows(me), own_sem.at[1])
    lengths_in = pltpu.make_async_copy(doc_lengths, lengths, own_sem.at[3])
    kv_load = pltpu.make_async_copy(kv_hbm, kv_raw, own_sem.at[4])
    q_load = pltpu.make_async_copy(q_hbm, q_raw, own_sem.at[5])
    kv_load.start()
    q_load.start()
    lengths_in.start()

    barrier = pltpu.get_barrier_semaphore()
    for step in range(1, heads):
        peer = (me + step) % heads
        pl.semaphore_signal(barrier, inc=1, device_id={"head": peer}, device_id_type=MESH)

    @pl.when(ctx != 0)
    def _():
        pl.semaphore_signal(barrier, inc=1, device_id={"ctx": beside}, device_id_type=MESH)

    @pl.when(jnp.logical_not(first))
    def _():
        pl.semaphore_signal(barrier, inc=1, device_id={"ctx": back}, device_id_type=MESH)

    window[:pad, :] = jnp.zeros((pad, window.shape[1]), window.dtype)

    @pl.when(first)
    def _():
        window[pad:pad + block, :] = jnp.zeros((block, window.shape[1]), window.dtype)

    @pl.when(ctx == 0)
    def _():
        window[pad + block:pad + REACH * block, :] = jnp.zeros(
            (block, window.shape[1]), window.dtype
        )

    onward = 1 - (ctx + REACH) // ctxs
    across = ((ctx + ctxs - 1) % ctxs + ctxs - 1) // ctxs
    kv_load.wait()
    kv_in[...] = jnp.swapaxes(kv_raw[...], 0, 1)
    own_kv.start()
    pl.semaphore_wait(barrier, heads - 1 + onward + across)

    for step in NEAR_FIRST:
        kv_copy(peer_at(me, step, heads, 1), me).start()

    q_load.wait()
    q_in[...] = jnp.swapaxes(q_raw[...], 0, 1)
    own_q.start()

    @pl.loop(0, heads - 1)
    def _(step):
        q_copy(peer_at(me, step, heads, 1), me).start()

    lengths_in.wait()

    @pl.loop(0, heads)
    def _(chunk):
        place = lax.broadcasted_iota(jnp.int32, (rows, TILE), 0) + (ctx * block + chunk * rows)
        start = jnp.zeros((rows, TILE), jnp.int32)
        end = jnp.int32(0)
        for doc in range(lengths.shape[0]):
            end = end + lengths[doc]
            start = jnp.where(place >= end, end, start)
        first_key[chunk] = start - ((ctx - REACH) * block + chunk * rows - pad)

    own_kv.wait()

    def pass_on(piece):
        @pl.when(jnp.logical_not(last))
        def _():
            z_copy(piece).start()

        @pl.when(odd == 0)
        def _():
            y_copy(piece).start()

    pass_on(me)
    for step in NEAR_FIRST:
        piece = peer_at(me, step, heads, -1)
        kv_copy(piece, piece).wait_recv()
        pass_on(piece)

    @pl.when(jnp.logical_not(first))
    def _():
        for step in (heads - 1, *NEAR_FIRST):
            piece = peer_at(me, step, heads, -1)
            z_copy(piece).wait_recv()

            @pl.when(odd == 1)
            def _():
                y_copy(piece).start()

    @pl.when(ctx >= 1)
    def _():
        @pl.loop(0, heads)
        def _(piece):
            y_copy(piece).wait_recv()

    own_q.wait()
    sharpness = HEAD_DIM ** -0.5 * LOG2E

    def chunk_of(step):
        return peer_at(me, step, heads, 1)

    def score(chunk, scores):
        packed = query_rows(chunk)[...]
        stacked = jnp.concatenate(
            [packed[:, j * HEAD_DIM:(j + 1) * HEAD_DIM] for j in range(GROUP)], axis=0
        )
        base = chunk * rows
        lowest = first_key[chunk]
        lane = lax.broadcasted_iota(jnp.int32, (rows, TILE), 1)
        row = lax.broadcasted_iota(jnp.int32, (rows, TILE), 0)
        top = None
        for tile in range(0, tiles, 2):
            width = min(2, tiles - tile) * TILE
            keys = window[pl.ds(pl.multiple_of(base + tile * TILE, 32), width), :HEAD_DIM]
            both = lax.dot_general(
                stacked, keys, (((1,), (1,)), ((), ())), preferred_element_type=jnp.float32
            )
            for half in range(width // TILE):
                part = both[:, half * TILE:(half + 1) * TILE]
                here = lane + (tile + half) * TILE
                kept = here >= lowest
                if (tile + half + 1) * TILE > pad + REACH * block:
                    kept = kept & (here <= row + (pad + REACH * block))
                part = jnp.where(kept[None], part.reshape(GROUP, rows, TILE), MASKED)
                part = part.reshape(GROUP * rows, TILE)
                scores[tile + half] = part
                top = part if top is None else jnp.maximum(top, part)
        return jnp.max(top, axis=1, keepdims=True)

    def mix(chunk, scores, top):
        base = chunk * rows
        total = None
        weights = []
        for tile in range(tiles):
            part = jnp.exp2((scores[tile] - top) * sharpness)
            total = part if total is None else total + part
            weights.append(part.astype(jnp.bfloat16))
        values = window[pl.ds(pl.multiple_of(base, 32), tiles * TILE), HEAD_DIM:]
        result = jnp.dot(
            jnp.concatenate(weights, axis=1), values, preferred_element_type=jnp.float32
        )
        total = jnp.sum(total, axis=1, keepdims=True)
        result = (result / total).astype(jnp.bfloat16)
        for j in range(GROUP):
            mixed[chunk, :, j * HEAD_DIM:(j + 1) * HEAD_DIM] = result[j * rows:(j + 1) * rows]

    def await_queries(step):
        @pl.when(step < heads - 1)
        def _():
            source = chunk_of(step)
            q_copy(source, source).wait_recv()

    def send_mixed(step):
        @pl.when(step < heads - 1)
        def _():
            o_copy(chunk_of(step), me).start()

    await_queries(0)
    tops[0] = score(chunk_of(0), scores_a)

    @pl.loop(0, heads, step=2)
    def _(step):
        await_queries(step + 1)
        tops[1] = score(chunk_of(step + 1), scores_b)
        mix(chunk_of(step), scores_a, tops[0])
        send_mixed(step)
        after = jnp.minimum(step + 2, heads - 1)
        await_queries(step + 2)
        tops[0] = score(chunk_of(after), scores_a)
        mix(chunk_of(step + 1), scores_b, tops[1])
        send_mixed(step + 1)

    own_out = pltpu.make_async_copy(mixed.at[me], out.at[me], own_sem.at[2])
    own_out.start()

    @pl.loop(0, heads - 1)
    def _(step):
        dest = (me + 1 + step) % heads
        kv_copy(dest, me).wait_send()
        q_copy(dest, me).wait_send()
        o_copy(dest, me).wait_send()
        o_copy(dest, dest).wait_recv()

    @pl.when(jnp.logical_not(last))
    def _():
        @pl.loop(0, heads)
        def _(piece):
            z_copy(piece).wait_send()

    @pl.when(ctx != 1)
    def _():
        @pl.loop(0, heads)
        def _(piece):
            y_copy(piece).wait_send()

    own_out.wait()


def local(heads, ctxs, queries, keyvals, doc_lengths):
    rows = queries.shape[0]
    block = heads * rows
    span = REACH * block + rows
    tiles = pl.cdiv(span, TILE)
    pad = tiles * TILE - span
    dma = pltpu.SemaphoreType.DMA((heads,))
    gathered = pl.pallas_call(
        functools.partial(attention_kernel, heads, ctxs),
        out_shape=jax.ShapeDtypeStruct((heads, rows, queries.shape[2]), jnp.bfloat16),
        in_specs=[
            pl.BlockSpec(memory_space=pltpu.HBM),
            pl.BlockSpec(memory_space=pltpu.HBM),
            pl.BlockSpec(memory_space=pltpu.HBM),
        ],
        out_specs=pl.BlockSpec(memory_space=pl.ANY),
        scratch_shapes=[
            pltpu.VMEM(queries.shape, jnp.bfloat16),
            pltpu.VMEM(keyvals.shape, jnp.bfloat16),
            pltpu.VMEM((heads, rows, queries.shape[2]), jnp.bfloat16),
            pltpu.VMEM((heads, rows, keyvals.shape[2]), jnp.bfloat16),
            pltpu.VMEM((pad + (REACH + 1) * block, keyvals.shape[2]), jnp.bfloat16),
            pltpu.VMEM((block, queries.shape[2]), jnp.bfloat16),
            pltpu.SMEM(doc_lengths.shape, jnp.int32),
            pltpu.VMEM((heads, rows, TILE), jnp.int32),
            pltpu.VMEM((tiles, GROUP * rows, TILE), jnp.float32),
            pltpu.VMEM((tiles, GROUP * rows, TILE), jnp.float32),
            pltpu.VMEM((2, GROUP * rows, 1), jnp.float32),
            pltpu.VMEM((heads, rows, queries.shape[2]), jnp.bfloat16),
            dma, dma, dma, dma, dma, dma, dma, dma, dma, dma,
            pltpu.SemaphoreType.DMA((6,)),
        ],
        compiler_params=pltpu.CompilerParams(collective_id=0, has_side_effects=True, vmem_limit_bytes=20 << 20),
    )(*(pltpu.with_memory_space_constraint(x, pltpu.HBM) for x in (doc_lengths, queries, keyvals)))
    return jnp.transpose(gathered, (1, 0, 2))


def solution(mesh):
    spec = P(("rep", "ctx", "head"), None, None)
    return jax.shard_map(
        functools.partial(local, mesh.shape["head"], mesh.shape["ctx"]),
        mesh=mesh,
        in_specs=(spec, spec, P("rep")),
        out_specs=spec,
        check_vma=False,
    )
```

```python
import functools

import jax
import jax.numpy as jnp
from jax import lax
from jax.experimental import pallas as pl
from jax.experimental.pallas import tpu as pltpu
from jax.sharding import PartitionSpec as P

GROUP = 4
HEAD_DIM = 128
REACH = 2
TILE = 128
MASKED = -1e30
LOG2E = 1.4426950408889634
MESH = pl.DeviceIdType.MESH


NEAR_FIRST = (6, 3, 5, 2, 4, 1, 0)


def peer_at(me, step, heads, way):
    pair = step // 2
    chips = heads // 2
    distance = chips // 2 + (1 - 2 * (pair % 2)) * ((pair + 1) // 2)
    flip = (step + pair // 3) % 2
    return 2 * ((me // 2 + chips + way * distance) % chips) + (me + flip) % 2


def attention_kernel(
    heads, ctxs, doc_lengths, q_hbm, kv_hbm, out, q_raw, kv_raw, q_in, kv_in, window, q_rows, lengths, first_key, scores_a, scores_b, tops, mixed,
    kv_send, kv_recv, q_send, q_recv, z_send, z_recv, y_send, y_recv, o_send, o_recv, own_sem,
):
    rows = q_in.shape[1]
    block = heads * rows
    me = lax.axis_index("head")
    ctx = lax.axis_index("ctx")
    odd = ctx % 2
    first = ctx < REACH
    last = ctx >= ctxs - REACH
    far = (ctx + REACH) % ctxs
    back = (ctx + ctxs - REACH) % ctxs
    beside = ctx + 1 - 2 * odd
    span = REACH * block + rows
    tiles = pl.cdiv(span, TILE)
    pad = tiles * TILE - span

    def key_rows(which, piece):
        return window.at[pl.ds(pl.multiple_of(pad + which * block + piece * rows, 32), rows), :]

    def query_rows(piece):
        return q_rows.at[pl.ds(pl.multiple_of(piece * rows, 32), rows), :]

    def kv_copy(dest, source):
        return pltpu.make_async_remote_copy(
            src_ref=kv_in.at[dest], dst_ref=key_rows(REACH, source),
            send_sem=kv_send.at[dest], recv_sem=kv_recv.at[source],
            device_id={"head": dest}, device_id_type=MESH,
        )

    def q_copy(dest, source):
        return pltpu.make_async_remote_copy(
            src_ref=q_in.at[dest], dst_ref=query_rows(source),
            send_sem=q_send.at[dest], recv_sem=q_recv.at[source],
            device_id={"head": dest}, device_id_type=MESH,
        )

    def z_copy(piece):
        return pltpu.make_async_remote_copy(
            src_ref=key_rows(REACH, piece), dst_ref=key_rows(0, piece),
            send_sem=z_send.at[piece], recv_sem=z_recv.at[piece],
            device_id={"ctx": far}, device_id_type=MESH,
        )

    def y_copy(piece):
        return pltpu.make_async_remote_copy(
            src_ref=key_rows(REACH * (1 - odd), piece), dst_ref=key_rows(1, piece),
            send_sem=y_send.at[piece], recv_sem=y_recv.at[piece],
            device_id={"ctx": beside}, device_id_type=MESH,
        )

    def o_copy(dest, source):
        return pltpu.make_async_remote_copy(
            src_ref=mixed.at[dest], dst_ref=out.at[source],
            send_sem=o_send.at[dest], recv_sem=o_recv.at[source],
            device_id={"head": dest}, device_id_type=MESH,
        )

    own_kv = pltpu.make_async_copy(kv_in.at[me], key_rows(REACH, me), own_sem.at[0])
    own_q = pltpu.make_async_copy(q_in.at[me], query_rows(me), own_sem.at[1])
    lengths_in = pltpu.make_async_copy(doc_lengths, lengths, own_sem.at[3])
    kv_load = pltpu.make_async_copy(kv_hbm, kv_raw, own_sem.at[4])
    q_load = pltpu.make_async_copy(q_hbm, q_raw, own_sem.at[5])
    kv_load.start()
    q_load.start()
    lengths_in.start()

    barrier = pltpu.get_barrier_semaphore()
    for step in range(1, heads):
        peer = (me + step) % heads
        pl.semaphore_signal(barrier, inc=1, device_id={"head": peer}, device_id_type=MESH)

    @pl.when(ctx != 0)
    def _():
        pl.semaphore_signal(barrier, inc=1, device_id={"ctx": beside}, device_id_type=MESH)

    @pl.when(jnp.logical_not(first))
    def _():
        pl.semaphore_signal(barrier, inc=1, device_id={"ctx": back}, device_id_type=MESH)

    window[:pad, :] = jnp.zeros((pad, window.shape[1]), window.dtype)

    @pl.when(first)
    def _():
        window[pad:pad + block, :] = jnp.zeros((block, window.shape[1]), window.dtype)

    @pl.when(ctx == 0)
    def _():
        window[pad + block:pad + REACH * block, :] = jnp.zeros(
            (block, window.shape[1]), window.dtype
        )

    onward = 1 - (ctx + REACH) // ctxs
    across = ((ctx + ctxs - 1) % ctxs + ctxs - 1) // ctxs
    kv_load.wait()
    kv_in[...] = jnp.swapaxes(kv_raw[...], 0, 1)
    own_kv.start()
    pl.semaphore_wait(barrier, heads - 1 + onward + across)

    for step in NEAR_FIRST:
        kv_copy(peer_at(me, step, heads, 1), me).start()

    own_kv.wait()

    def pass_on(piece):
        @pl.when(jnp.logical_not(last))
        def _():
            z_copy(piece).start()

        @pl.when(odd == 0)
        def _():
            y_copy(piece).start()

    pass_on(me)

    q_load.wait()
    q_in[...] = jnp.swapaxes(q_raw[...], 0, 1)
    own_q.start()

    @pl.loop(0, heads - 1)
    def _(step):
        q_copy(peer_at(me, step, heads, 1), me).start()

    lengths_in.wait()

    @pl.loop(0, heads)
    def _(chunk):
        place = lax.broadcasted_iota(jnp.int32, (rows, TILE), 0) + (ctx * block + chunk * rows)
        start = jnp.zeros((rows, TILE), jnp.int32)
        end = jnp.int32(0)
        for doc in range(lengths.shape[0]):
            end = end + lengths[doc]
            start = jnp.where(place >= end, end, start)
        first_key[chunk] = start - ((ctx - REACH) * block + chunk * rows - pad)

    for step in NEAR_FIRST:
        piece = peer_at(me, step, heads, -1)
        kv_copy(piece, piece).wait_recv()
        pass_on(piece)

    @pl.when(jnp.logical_not(first))
    def _():
        for step in (heads - 1, *NEAR_FIRST):
            piece = peer_at(me, step, heads, -1)
            z_copy(piece).wait_recv()

            @pl.when(odd == 1)
            def _():
                y_copy(piece).start()

    @pl.when(ctx >= 1)
    def _():
        @pl.loop(0, heads)
        def _(piece):
            y_copy(piece).wait_recv()

    own_q.wait()
    sharpness = HEAD_DIM ** -0.5 * LOG2E

    def chunk_of(step):
        return peer_at(me, step, heads, 1)

    def score(chunk, scores):
        packed = query_rows(chunk)[...]
        stacked = jnp.concatenate(
            [packed[:, j * HEAD_DIM:(j + 1) * HEAD_DIM] for j in range(GROUP)], axis=0
        )
        base = chunk * rows
        lowest = first_key[chunk]
        lane = lax.broadcasted_iota(jnp.int32, (rows, TILE), 1)
        row = lax.broadcasted_iota(jnp.int32, (rows, TILE), 0)
        top = None
        for tile in range(0, tiles, 2):
            width = min(2, tiles - tile) * TILE
            keys = window[pl.ds(pl.multiple_of(base + tile * TILE, 32), width), :HEAD_DIM]
            both = lax.dot_general(
                stacked, keys, (((1,), (1,)), ((), ())), preferred_element_type=jnp.float32
            )
            for half in range(width // TILE):
                part = both[:, half * TILE:(half + 1) * TILE]
                here = lane + (tile + half) * TILE
                kept = here >= lowest
                if (tile + half + 1) * TILE > pad + REACH * block:
                    kept = kept & (here <= row + (pad + REACH * block))
                part = jnp.where(kept[None], part.reshape(GROUP, rows, TILE), MASKED)
                part = part.reshape(GROUP * rows, TILE)
                scores[tile + half] = part
                top = part if top is None else jnp.maximum(top, part)
        return jnp.max(top, axis=1, keepdims=True)

    def mix(chunk, scores, top):
        base = chunk * rows
        total = None
        weights = []
        for tile in range(tiles):
            part = jnp.exp2((scores[tile] - top) * sharpness)
            total = part if total is None else total + part
            weights.append(part.astype(jnp.bfloat16))
        values = window[pl.ds(pl.multiple_of(base, 32), tiles * TILE), HEAD_DIM:]
        result = jnp.dot(
            jnp.concatenate(weights, axis=1), values, preferred_element_type=jnp.float32
        )
        total = jnp.sum(total, axis=1, keepdims=True)
        result = (result / total).astype(jnp.bfloat16)
        for j in range(GROUP):
            mixed[chunk, :, j * HEAD_DIM:(j + 1) * HEAD_DIM] = result[j * rows:(j + 1) * rows]

    def await_queries(step):
        @pl.when(step < heads - 1)
        def _():
            source = chunk_of(step)
            q_copy(source, source).wait_recv()

    def send_mixed(step):
        @pl.when(step < heads - 1)
        def _():
            o_copy(chunk_of(step), me).start()

    await_queries(0)
    tops[0] = score(chunk_of(0), scores_a)

    @pl.loop(0, heads, step=2)
    def _(step):
        await_queries(step + 1)
        tops[1] = score(chunk_of(step + 1), scores_b)
        mix(chunk_of(step), scores_a, tops[0])
        send_mixed(step)
        after = jnp.minimum(step + 2, heads - 1)
        await_queries(step + 2)
        tops[0] = score(chunk_of(after), scores_a)
        mix(chunk_of(step + 1), scores_b, tops[1])
        send_mixed(step + 1)

    own_out = pltpu.make_async_copy(mixed.at[me], out.at[me], own_sem.at[2])
    own_out.start()

    @pl.loop(0, heads - 1)
    def _(step):
        dest = (me + 1 + step) % heads
        kv_copy(dest, me).wait_send()
        q_copy(dest, me).wait_send()
        o_copy(dest, me).wait_send()
        o_copy(dest, dest).wait_recv()

    @pl.when(jnp.logical_not(last))
    def _():
        @pl.loop(0, heads)
        def _(piece):
            z_copy(piece).wait_send()

    @pl.when(ctx != 1)
    def _():
        @pl.loop(0, heads)
        def _(piece):
            y_copy(piece).wait_send()

    own_out.wait()


def local(heads, ctxs, queries, keyvals, doc_lengths):
    rows = queries.shape[0]
    block = heads * rows
    span = REACH * block + rows
    tiles = pl.cdiv(span, TILE)
    pad = tiles * TILE - span
    dma = pltpu.SemaphoreType.DMA((heads,))
    gathered = pl.pallas_call(
        functools.partial(attention_kernel, heads, ctxs),
        out_shape=jax.ShapeDtypeStruct((heads, rows, queries.shape[2]), jnp.bfloat16),
        in_specs=[
            pl.BlockSpec(memory_space=pltpu.HBM),
            pl.BlockSpec(memory_space=pltpu.HBM),
            pl.BlockSpec(memory_space=pltpu.HBM),
        ],
        out_specs=pl.BlockSpec(memory_space=pl.ANY),
        scratch_shapes=[
            pltpu.VMEM(queries.shape, jnp.bfloat16),
            pltpu.VMEM(keyvals.shape, jnp.bfloat16),
            pltpu.VMEM((heads, rows, queries.shape[2]), jnp.bfloat16),
            pltpu.VMEM((heads, rows, keyvals.shape[2]), jnp.bfloat16),
            pltpu.VMEM((pad + (REACH + 1) * block, keyvals.shape[2]), jnp.bfloat16),
            pltpu.VMEM((block, queries.shape[2]), jnp.bfloat16),
            pltpu.SMEM(doc_lengths.shape, jnp.int32),
            pltpu.VMEM((heads, rows, TILE), jnp.int32),
            pltpu.VMEM((tiles, GROUP * rows, TILE), jnp.float32),
            pltpu.VMEM((tiles, GROUP * rows, TILE), jnp.float32),
            pltpu.VMEM((2, GROUP * rows, 1), jnp.float32),
            pltpu.VMEM((heads, rows, queries.shape[2]), jnp.bfloat16),
            dma, dma, dma, dma, dma, dma, dma, dma, dma, dma,
            pltpu.SemaphoreType.DMA((6,)),
        ],
        compiler_params=pltpu.CompilerParams(collective_id=0, has_side_effects=True, vmem_limit_bytes=20 << 20),
    )(*(pltpu.with_memory_space_constraint(x, pltpu.HBM) for x in (doc_lengths, queries, keyvals)))
    return jnp.transpose(gathered, (1, 0, 2))


def solution(mesh):
    spec = P(("rep", "ctx", "head"), None, None)
    return jax.shard_map(
        functools.partial(local, mesh.shape["head"], mesh.shape["ctx"]),
        mesh=mesh,
        in_specs=(spec, spec, P("rep")),
        out_specs=spec,
        check_vma=False,
    )
```
